32 devices in a mesh: groups: 2 (over y), mem: 4 (over z), head: 2 (over x), width: 2 (over core).
Axes of the slice: x: 2, y: 2, z: 4, core: 2. Of those that a mesh axis runs over, the one named last changes fastest.
Arguments:
- residual_in: bfloat16 [64, 5120], P('groups', 'mem'), parts along dimension 0, may hold values from -26 to 26
- attention_gain: float32 [5120], P('mem'), may hold values from 0.5 to 1.5
- query_weight: bfloat16 [5120, 8192], P('mem', ('head', 'width')), may hold values from -0.078125 to 0.078125
- key_weight: bfloat16 [5120, 1024], P('mem', ('head', 'width')), may hold values from -0.078125 to 0.078125
- value_weight: bfloat16 [5120, 1024], P('mem', ('head', 'width')), may hold values from -0.078125 to 0.078125
- query_norm: float32 [128], replicated, may hold values from 0.25 to 1.75
- key_norm: float32 [128], replicated, may hold values from 0.1 to 1.9
- cache_keys: bfloat16 [65536, 8, 128], P(('groups', 'mem'), ('head', 'width')), parts along dimension 0, may hold values from -480 to 480
- cache_values: bfloat16 [65536, 8, 128], P(('groups', 'mem'), ('head', 'width')), parts along dimension 0, may hold values from -12 to 12
- slot_request: int32 [65536], P(('groups', 'mem')), parts along dimension 0, may hold values from 0 to 16, as said below
- lengths: int32 [32], P('groups'), parts along dimension 0, may hold values from 1056 to 1760, as said below
- output_weight: bfloat16 [8192, 5120], P(('head', 'width'), 'mem'), may hold values from -0.0625 to 0.0625
- second_gain: float32 [5120], P('mem'), may hold values from 0.5 to 1.5
- gate_weight: bfloat16 [5120, 25600], P('mem', ('head', 'width')), may hold values from -0.078125 to 0.078125
- up_weight: bfloat16 [5120, 25600], P('mem', ('head', 'width')), may hold values from -0.078125 to 0.078125
- down_weight: bfloat16 [25600, 5120], P(('head', 'width'), 'mem'), may hold values from -0.0390625 to 0.0390625
Outputs:
- layer_out: bfloat16 [64, 5120], P('groups', 'mem'), parts along dimension 0
The draws below stay inside these ranges and needn't reach their ends.
There are 2 independent parts, one for each index of `groups`. The reference program is written for one: setup_inputs(seed, part) draws one part's arguments, and reference() takes and returns one part's arrays. A program takes and returns all parts, laid end to end along the dimension named above; an argument that names none is the same for every part. Nothing has to cross between parts.
Inputs may be any that keep to these rules, and one draw needn't show every extreme that they name: slot_request[s] names the request whose cached token sits in slot s, or is 16 for an empty slot. On each owner (each aligned block of 8192 slots along mem) the used slots come first; taking owners in order and their used slots in order, requests 0 to 15 follow one another in consecutive slots, so a request may continue on the next owner, but on no further one: a request's slots lie on at most two consecutive owners. Request r has exactly lengths[r] slots. Some owner has all its slots used. lengths[r] is the number of cached tokens of request r; its new tokens stand at positions lengths[r] and lengths[r] + 1.
All inputs are finite; a program needn't handle non-finite values.
Results may differ from the reference program's by a relative error of at most 0.0095.
The reference program's roundings to bfloat16 on the way count: a program that leaves them out, or rounds other values in their place, can miss the bound.
Values may be sent and summed in bfloat16 or wider, within the bound.
A program may use at most 128 MiB of HBM per device.

```python
import math
import jax
import jax.numpy as jnp
from jax import lax

D = 5120
HEADS = 64
KV_HEADS = 8
HEAD_DIM = 128
FF = 25600
CAP = 8192
REQ_DEV = 4
REQUESTS = 16
TOKENS = 32
SLOTS = 32768
N_MEM = 4


def request_layout(key):
    layout_key = jax.random.fold_in(key, 17)
    order_key, pair_key, sign_key, chosen_key = jax.random.split(layout_key, 4)
    unit_slots = CAP // 16
    ranking = jax.random.permutation(order_key, N_MEM)
    shares = jnp.where(ranking < N_MEM // 2, 16, 6).astype(jnp.int32)
    filled = (shares * unit_slots).astype(jnp.int32)
    middle_length = 11 * CAP // (16 * REQ_DEV)
    spread = middle_length // 4
    pair_count = REQUESTS // 2
    excess = jax.random.randint(pair_key, (pair_count,), 0, spread + 1)
    chosen = jax.random.randint(chosen_key, (), 0, pair_count)
    excess = jnp.where(jnp.arange(pair_count, dtype=jnp.int32) == chosen, spread, excess)
    signs = 2 * jax.random.randint(sign_key, (pair_count,), 0, 2) - 1
    signed = (excess * signs).astype(jnp.int32)
    lengths = jnp.stack([middle_length + signed, middle_length - signed], axis=1).reshape(REQUESTS).astype(jnp.int32)
    borders = jnp.cumsum(lengths)[:-1].astype(jnp.int32)
    starts = jnp.cumsum(filled) - filled
    slot_index = jnp.arange(SLOTS, dtype=jnp.int32)
    owner_of = slot_index // CAP
    within = slot_index % CAP
    occupied = within < filled[owner_of]
    stream = starts[owner_of] + within
    request = jnp.sum((borders[None, :] <= stream[:, None]).astype(jnp.int32), axis=1)
    return (lengths, jnp.where(occupied, request, REQUESTS).astype(jnp.int32))


def draw_lengths(key, part):
    return request_layout(key)[0]


def draw_slot_request(key, part):
    return request_layout(key)[1]


def projection_pair(key):
    pair_key = jax.random.fold_in(key, 41)
    query_key, other_key = jax.random.split(pair_key)
    group_size = HEADS // KV_HEADS
    drawn_query = jnp.clip(jax.random.normal(query_key, (D, KV_HEADS, group_size, HEAD_DIM), jnp.float32), -5.0, 5.0)
    independent = jnp.clip(jax.random.normal(other_key, (D, KV_HEADS, HEAD_DIM), jnp.float32), -5.0, 5.0)
    unit_scale = 1.0 / math.sqrt(D)
    linked = 0.8 * drawn_query[:, :, 0, :] + 0.6 * independent
    query_cols = jnp.clip(drawn_query * unit_scale, -0.078125, 0.078125).reshape(D, HEADS * HEAD_DIM)
    key_cols = jnp.clip(linked * unit_scale, -0.078125, 0.078125).reshape(D, KV_HEADS * HEAD_DIM)
    return (query_cols.astype(jnp.bfloat16), key_cols.astype(jnp.bfloat16))


def draw_query_weight(key, part):
    return projection_pair(key)[0]


def draw_key_weight(key, part):
    return projection_pair(key)[1]


def draw_cache_keys(key, part):
    normal_key = jax.random.fold_in(jax.random.fold_in(key, 29), 0)
    values = jnp.clip(jax.random.normal(normal_key, (SLOTS, KV_HEADS, HEAD_DIM), jnp.float32), -6.0, 6.0)
    return values.astype(jnp.bfloat16)


def draw_residual_in(key, part):
    base_key, column_key, row_key = jax.random.split(jax.random.fold_in(key, 3), 3)
    ramp = 0.15 + 1.35 * jnp.arange(D, dtype=jnp.float32) / (D - 1)
    columns = ramp * jnp.exp(jax.random.uniform(column_key, (D,), jnp.float32, -0.3, 0.3))
    values = jnp.clip(jax.random.normal(base_key, (TOKENS, D), jnp.float32), -5.0, 5.0)
    rows = jnp.exp(jax.random.uniform(row_key, (TOKENS, 1), jnp.float32, -1.5, 0.5))
    return (values * columns * rows).astype(jnp.bfloat16)


def steps_of(own_key, dims, cuts, least, top_value):
    loudness, own = 1.0, jax.random.fold_in(own_key, 6)
    for position, shards_of in cuts:
        draws = jnp.exp(jax.random.uniform(jax.random.fold_in(own, position), (shards_of,), jnp.float32, least / len(cuts), top_value / len(cuts)))
        loudness = loudness * jnp.repeat(draws, dims[position] // shards_of).reshape([-1 if axis == position else 1 for axis in range(len(dims))])
    return loudness


def gaussian(rng, shape, width, bound, cuts=(), kind=jnp.bfloat16):
    drawn = jax.random.normal(rng, shape, jnp.float32) * width
    if len(cuts) > 0:
        drawn = steps_of(rng, shape, cuts, -0.22, 0.18) * drawn
    return jnp.clip(drawn, min=-bound, max=bound).astype(kind)


def setup_inputs(seed: int = 0, part: int = 0) -> dict:
    key_of = jax.random.split(jax.random.key(seed), 17)
    own_keys = jax.random.split(jax.random.fold_in(key_of[16], part), 17)
    return {
        "residual_in": draw_residual_in(jax.random.fold_in(jax.random.fold_in(key_of[16], part), 71), part),
        "attention_gain": jnp.clip(1.0 + 0.1 * jax.random.normal(key_of[1], (D,), jnp.float32), 0.5, 1.5),
        "query_weight": draw_query_weight(jax.random.fold_in(key_of[16], 71), part),
        "key_weight": draw_key_weight(jax.random.fold_in(key_of[16], 71), part),
        "value_weight": gaussian(key_of[4], (D, KV_HEADS * HEAD_DIM), D ** -0.5, 0.078125, ((0, 4), (1, 4))),
        "query_norm": jnp.clip(1.0 + 0.15 * jax.random.normal(key_of[5], (HEAD_DIM,), jnp.float32), 0.25, 1.75),
        "key_norm": jnp.clip(1.0 + 0.18 * jax.random.normal(key_of[6], (HEAD_DIM,), jnp.float32), 0.1, 1.9),
        "cache_keys": draw_cache_keys(jax.random.fold_in(jax.random.fold_in(key_of[16], part), 71), part),
        "cache_values": gaussian(own_keys[8], (SLOTS, KV_HEADS, HEAD_DIM), 2.0, 12.0, ((0, 4), (1, 4))),
        "slot_request": draw_slot_request(jax.random.fold_in(jax.random.fold_in(key_of[16], part), 71), part),
        "lengths": draw_lengths(jax.random.fold_in(jax.random.fold_in(key_of[16], part), 71), part),
        "output_weight": gaussian(key_of[11], (HEADS * HEAD_DIM, D), (HEADS * HEAD_DIM) ** -0.5, 0.0625, ((0, 4), (1, 4))),
        "second_gain": jnp.clip(1.0 + 0.1 * jax.random.normal(key_of[12], (D,), jnp.float32), 0.5, 1.5),
        "gate_weight": gaussian(key_of[13], (D, FF), D ** -0.5, 0.078125, ((0, 4), (1, 4))),
        "up_weight": gaussian(key_of[14], (D, FF), D ** -0.5, 0.078125, ((0, 4), (1, 4))),
        "down_weight": gaussian(key_of[15], (FF, D), FF ** -0.5, 0.0390625, ((0, 4), (1, 4))),
    }


epsilon = 1e-06
rope_base = 1000000.0
floor_score = -1e+30

def rotate(values, places):
    breadth = values.shape[-1]
    halfway = breadth // 2
    frequency = rope_base ** (-(jnp.arange(halfway, dtype=jnp.float32) * 2.0) / breadth)
    angles = places[..., None] * frequency
    cosine = jnp.cos(angles)
    sine_part = jnp.sin(angles)
    leading = values[..., :halfway]
    trailing = values[..., halfway:]
    return jnp.concatenate([leading * cosine - trailing * sine_part, trailing * cosine + leading * sine_part], axis=-1)

def head_norm(values, scaling):
    mean_square = lax.optimization_barrier(jnp.mean(values * values, axis=-1, keepdims=True))
    return values * lax.rsqrt(mean_square + epsilon) * scaling

def reference(residual_in, attention_gain, query_weight, key_weight, value_weight, query_norm, key_norm, cache_keys, cache_values, slot_request, lengths, output_weight, second_gain, gate_weight, up_weight, down_weight):
    row_count = TOKENS
    requests = REQUESTS
    group_size = HEADS // KV_HEADS
    score_scale = 1.0 / math.sqrt(HEAD_DIM)
    residual = residual_in.astype(jnp.float32)
    normed = head_norm(residual, attention_gain).astype(jnp.bfloat16)
    offsets = jnp.arange(2, dtype=jnp.int32)
    places = (lengths[:, None] + offsets[None, :]).reshape(row_count).astype(jnp.float32)
    query_full = jnp.dot(normed, query_weight, preferred_element_type=jnp.float32).reshape(row_count, HEADS, HEAD_DIM)
    key_full = jnp.dot(normed, key_weight, preferred_element_type=jnp.float32).reshape(row_count, KV_HEADS, HEAD_DIM)
    value_full = jnp.dot(normed, value_weight, preferred_element_type=jnp.float32).reshape(row_count, KV_HEADS, HEAD_DIM)
    queries = rotate(head_norm(query_full, query_norm), places[:, None]).astype(jnp.bfloat16)
    new_keys = rotate(head_norm(key_full, key_norm), places[:, None]).astype(jnp.bfloat16)
    new_values = value_full.astype(jnp.bfloat16)
    query_pairs = queries.reshape(requests, 2, KV_HEADS, group_size, HEAD_DIM).astype(jnp.float32)
    key_pairs = new_keys.reshape(requests, 2, KV_HEADS, HEAD_DIM).astype(jnp.float32)
    value_pairs = new_values.reshape(requests, 2, KV_HEADS, HEAD_DIM).astype(jnp.float32)
    allowed = (offsets[None, :] <= offsets[:, None])[None, :, None, None, :]
    own_scores = jnp.einsum('rtkgd,rskd->rtkgs', query_pairs, key_pairs) * score_scale
    own_scores = jnp.where(allowed, own_scores, floor_score)
    key_owners = cache_keys.reshape(N_MEM, CAP, KV_HEADS, HEAD_DIM)
    value_owners = cache_values.reshape(N_MEM, CAP, KV_HEADS, HEAD_DIM)
    slot_owners = slot_request.reshape(N_MEM, CAP)

    def per_head(head_index):
        query_head = lax.dynamic_index_in_dim(query_pairs, head_index, 2, keepdims=False)
        own_head = lax.dynamic_index_in_dim(own_scores, head_index, 2, keepdims=False)
        value_head = lax.dynamic_index_in_dim(value_pairs, head_index, 2, keepdims=False)

        def slot_scores(key_block, owner_block):
            picked = jnp.take(query_head, jnp.minimum(owner_block, requests - 1).astype(jnp.int32), axis=0)
            key_head = lax.dynamic_index_in_dim(key_block, head_index, 1, keepdims=False).astype(jnp.float32)
            return jnp.einsum('stgd,sd->stg', picked, key_head) * score_scale

        def find_top(highest, items):
            key_block, owner_block = items
            scores = slot_scores(key_block, owner_block)
            block_top = jax.ops.segment_max(scores, owner_block, num_segments=requests + 1)
            return (jnp.maximum(highest, block_top), None)
        start_top = jnp.full((requests + 1, 2, group_size), floor_score, jnp.float32)
        cache_top, unused = lax.scan(find_top, start_top, (key_owners, slot_owners))
        highest = jnp.maximum(cache_top[:requests], lax.optimization_barrier(jnp.max(own_head, axis=-1)))
        padded_top = jnp.concatenate([highest, jnp.zeros((1, 2, group_size), jnp.float32)], axis=0)

        def gather_sums(carried, items):
            summed, running = carried
            key_block, value_block, owner_block = items
            scores = slot_scores(key_block, owner_block)
            weights = jnp.exp(scores - jnp.take(padded_top, owner_block, axis=0))
            weights = jnp.where((owner_block < requests)[:, None, None], weights, 0.0)
            value_slice = lax.dynamic_index_in_dim(value_block, head_index, 1, keepdims=False).astype(jnp.float32)
            rounded = lax.optimization_barrier(weights.astype(jnp.bfloat16)).astype(jnp.float32)
            terms = rounded[..., None] * value_slice[:, None, None, :]
            summed = summed + jax.ops.segment_sum(weights, owner_block, num_segments=requests + 1)
            running = running + jax.ops.segment_sum(terms, owner_block, num_segments=requests + 1)
            return ((summed, running), None)
        start_sums = (jnp.zeros((requests + 1, 2, group_size), jnp.float32), jnp.zeros((requests + 1, 2, group_size, HEAD_DIM), jnp.float32))
        sums_out, unused_two = lax.scan(gather_sums, start_sums, (key_owners, value_owners, slot_owners))
        summed, running = sums_out
        own_weights = jnp.where(allowed[:, :, 0], jnp.exp(own_head - highest[..., None]), 0.0)
        own_rounded = lax.optimization_barrier(own_weights.astype(jnp.bfloat16)).astype(jnp.float32)
        summed = summed[:requests] + lax.optimization_barrier(jnp.sum(own_weights, axis=-1))
        running = running[:requests] + jnp.einsum('rtgs,rsd->rtgd', own_rounded, value_head)
        return running / summed[..., None]
    attended = lax.map(per_head, jnp.arange(KV_HEADS, dtype=jnp.int32))
    attended = jnp.transpose(attended, (1, 2, 0, 3, 4)).reshape(row_count, HEADS * HEAD_DIM).astype(jnp.bfloat16)
    projected = jnp.dot(attended, output_weight, preferred_element_type=jnp.float32)
    middle = (residual + projected).astype(jnp.bfloat16)
    middle_wide = middle.astype(jnp.float32)
    normed_mid = head_norm(middle_wide, second_gain).astype(jnp.bfloat16)
    gate_lin = jnp.dot(normed_mid, gate_weight, preferred_element_type=jnp.float32)
    up_lin = jnp.dot(normed_mid, up_weight, preferred_element_type=jnp.float32)
    activated = (jax.nn.silu(gate_lin) * up_lin).astype(jnp.bfloat16)
    down_sum = jnp.dot(activated, down_weight, preferred_element_type=jnp.float32)
    return (middle_wide + down_sum).astype(jnp.bfloat16)
```

```python
import functools
import math

import jax
import jax.numpy as jnp
from jax import lax
from jax.experimental import pallas as pl
from jax.experimental.pallas import tpu as pltpu
from jax.sharding import PartitionSpec as P

epsilon = 1e-06
rope_base = 1000000.0
floor_score = -1e30
LANES = 128
CHUNK = 1792
VMEM_LIMIT = 67043328
f32 = jnp.float32
bf16 = jnp.bfloat16


def tile_of(size, most):
    best = LANES
    for t in range(LANES, most + 1, LANES):
        if size % t == 0:
            best = t
    return best


class Ring:
    def __init__(self, axes, sizes):
        self.axes, self.sizes = axes, sizes
        self.n = math.prod(sizes)
        self.me = 0
        for axis, size in zip(axes, sizes):
            self.me = self.me * size + lax.axis_index(axis)

    def peer(self, d):
        return lax.rem(self.me + d, self.n)

    def ident(self, p):
        if len(self.axes) == 1:
            return {self.axes[0]: p}
        return {self.axes[0]: p // self.sizes[1], self.axes[1]: p % self.sizes[1]}

    def order(self):
        half = self.n // 2
        return sorted(range(1, self.n), key=lambda d: abs(d - half))

    def greet(self, barrier):
        for d in range(1, self.n):
            pl.semaphore_signal(
                barrier, inc=1, device_id=self.ident(self.peer(d)),
                device_id_type=pl.DeviceIdType.MESH,
            )

    def copies(self, src, dst, send, recv):
        out = []
        for d in self.order():
            p = self.peer(d)
            out.append(
                pltpu.make_async_remote_copy(
                    src_ref=src(p), dst_ref=dst(d), send_sem=send(d - 1), recv_sem=recv(d - 1),
                    device_id=self.ident(p), device_id_type=pl.DeviceIdType.MESH,
                )
            )
        return out


def start_all(copies):
    for c in copies:
        c.start()


def recv_all(copies):
    for c in copies:
        c.wait_recv()


def send_all(copies):
    for c in copies:
        c.wait_send()


def qkv_kernel(
    n, q_here, kv_here, res_ref, gain_ref, qn_ref, kn_ref, cos_ref, sin_ref, wq, wk, wv, out_ref,
    w, sq, sqr, part, partr, gath, wsem, s0, r0, s1, r1, s2, r2,
):
    ring = Ring(("mem",), (n,))
    rows, dl = res_ref.shape
    rn, cols = part.shape[1], part.shape[2]
    cq, ck = wq.shape[1], wk.shape[1]
    loads = [
        pltpu.make_async_copy(wq, w.at[:, pl.ds(0, cq)], wsem.at[0]),
        pltpu.make_async_copy(wk, w.at[:, pl.ds(cq, ck)], wsem.at[1]),
        pltpu.make_async_copy(wv, w.at[:, pl.ds(cq + ck, ck)], wsem.at[2]),
    ]
    start_all(loads)
    res = res_ref[...].astype(f32)
    sums = jnp.sum(res * res, axis=1, keepdims=True)
    sq[...] = jnp.broadcast_to(sums, sq.shape)
    barrier = pltpu.get_barrier_semaphore()
    ring.greet(barrier)
    pl.semaphore_wait(barrier, n - 1)
    c0 = ring.copies(lambda p: sq, lambda d: sqr.at[d - 1], lambda i: s0.at[i], lambda i: r0.at[i])
    start_all(c0)
    recv_all(c0)
    total = sq[...]
    for d in range(n - 1):
        total = total + sqr[d]
    scale = lax.rsqrt(total / (dl * n) + epsilon)[:, :1]
    normed = (res * scale * gain_ref[...]).astype(bf16)
    for c in loads:
        c.wait()
    tn = tile_of(cols, 640)
    for t in range(cols // tn):
        block = jnp.dot(normed, w[:, t * tn : (t + 1) * tn], preferred_element_type=f32)
        part[:, :, t * tn : (t + 1) * tn] = block.reshape(n, rn, tn)
    c1 = ring.copies(
        lambda p: part.at[p], lambda d: partr.at[d - 1], lambda i: s1.at[i], lambda i: r1.at[i]
    )
    start_all(c1)
    recv_all(c1)
    here = pl.ds(ring.me * rn, rn)
    cosine, sine = cos_ref[here, :], sin_ref[here, :]
    for h in range(q_here + 2 * kv_here):
        span = slice(h * LANES, (h + 1) * LANES)
        x = part[ring.me, :, span]
        for d in range(n - 1):
            x = x + partr[d, :, span]
        if h < q_here + kv_here:
            gain = qn_ref[...] if h < q_here else kn_ref[...]
            square = jnp.mean(x * x, axis=-1, keepdims=True)
            x = x * lax.rsqrt(square + epsilon) * gain
            x = x * cosine + pltpu.roll(x, LANES // 2, 1) * sine
        gath[ring.me, :, span] = x.astype(bf16)
    c2 = ring.copies(
        lambda p: gath.at[ring.me], lambda d: gath.at[ring.me],
        lambda i: s2.at[i], lambda i: r2.at[i],
    )
    start_all(c2)
    recv_all(c2)
    out_ref[...] = gath[...]
    send_all(c0 + c1 + c2)


def attend_kernel(
    n, kv, starts, ends, q_ref, nk_ref, nv_ref, k_ref, v_ref, o_ref, st_ref, lse,
):
    requests, m_rows, hd = q_ref.shape
    q_here = m_rows // 2
    group = q_here // kv
    cap = k_ref.shape[0] // kv
    chunk = min(CHUNK, cap)
    rpc = requests // n
    me = lax.axis_index("mem")
    score_scale = 1.0 / math.sqrt(hd)
    row = lax.broadcasted_iota(jnp.int32, (m_rows, chunk * kv), 0)
    col = lax.broadcasted_iota(jnp.int32, (m_rows, chunk * kv), 1)
    same = ((row // group) % kv) == (col % kv)

    def visit(r, unused):
        s, e = starts[r], ends[r]
        q = q_ref[r]
        qf = q.astype(f32)
        mine = (r // rpc) == me
        keys, vals = nk_ref[r], nv_ref[r]
        tops, sums, accs = [], [], []
        for t in range(2):
            for k in range(kv):
                b = (t * kv + k) * group
                qb = qf[b : b + group]
                sc = [
                    jnp.sum(qb * keys[u * kv + k : u * kv + k + 1], axis=-1, keepdims=True)
                    * score_scale
                    for u in range(t + 1)
                ]
                top = sc[0] if t == 0 else jnp.maximum(sc[0], sc[1])
                ws = [jnp.exp(x - top) for x in sc]
                total, acc = 0.0, 0.0
                for u, x in enumerate(ws):
                    total = total + x
                    acc = acc + x.astype(bf16).astype(f32) * vals[u * kv + k : u * kv + k + 1]
                tops.append(top)
                sums.append(total)
                accs.append(acc)
        top = jnp.where(mine, jnp.concatenate(tops, axis=0), floor_score)
        total = jnp.where(mine, jnp.concatenate(sums, axis=0), 0.0)
        acc = jnp.where(mine, jnp.concatenate(accs, axis=0), 0.0)
        base = (s // 16) * 16
        trips = jnp.where(e > s, (e - base + chunk - 1) // chunk, 0)

        def step(c, carried):
            top, total, acc = carried
            want = base + c * chunk
            at = jnp.minimum(want, cap - chunk)
            low = jnp.maximum(s, want)
            span = pl.ds(pl.multiple_of(at * kv, 16), chunk * kv)
            scores = (
                lax.dot_general(
                    q, k_ref[span, :], (((1,), (1,)), ((), ())), preferred_element_type=f32
                )
                * score_scale
            )
            valid = same & (col >= (low - at) * kv) & (col < (e - at) * kv)
            scores = jnp.where(valid, scores, floor_score)
            new = jnp.maximum(top, jnp.max(scores, axis=-1, keepdims=True))
            weights = jnp.exp(scores - new)
            factor = jnp.exp(top - new)
            total = total * factor + jnp.sum(weights, axis=-1, keepdims=True)
            acc = acc * factor + jnp.dot(
                weights.astype(bf16), v_ref[span, :], preferred_element_type=f32
            )
            return new, total, acc

        top, total, acc = lax.fori_loop(0, trips, step, (top, total, acc))
        some = total > 0.0
        safe = jnp.where(some, total, 1.0)
        o_ref[r] = acc / safe
        lse[r] = jnp.broadcast_to(jnp.where(some, top + jnp.log(safe), floor_score), (m_rows, LANES))
        return unused

    lax.fori_loop(0, requests, visit, 0)
    for j in range(n):
        flat = lse[j * rpc : (j + 1) * rpc].reshape(rpc * m_rows, LANES)
        st_ref[j] = flat.T[:8]


def tail_kernel(
    n, hwn, q_here, o_ref, st_ref, res_ref, gain_ref, wo_h, wg_h, wu_h, wd_h, out_ref,
    wo, wg, wu, wd, osend, orecv, strecv, flat, att, opart, orow, midn, sq, sqr,
    gsend, grecv, gown, act, dpart, drecv, fin,
    wosem, wgsem, wusem, wdsem,
    sa, ra, sb, rb, sc, rc, sd, rd, se, re, sf, rf, sg, rg, sh, rh, si, ri, sj, rj,
):
    mem = Ring(("mem",), (n,))
    hw = Ring(("head", "width"), hwn)
    nh = hw.n
    tiles, dl, tn = wg.shape
    rn = att.shape[1]
    rh_rows = midn.shape[1]
    per = flat.shape[0]
    load_o = pltpu.make_async_copy(wo_h, wo, wosem)
    load_o.start()

    def gate_load(t):
        span = pl.ds(pl.multiple_of(t * tn, LANES), tn)
        return (
            pltpu.make_async_copy(wg_h.at[:, span], wg.at[t], wgsem.at[t]),
            pltpu.make_async_copy(wu_h.at[:, span], wu.at[t], wusem.at[t]),
        )

    def down_load(t):
        span = pl.ds(pl.multiple_of(t * tn, LANES), tn)
        return pltpu.make_async_copy(wd_h.at[span, :], wd.at[t], wdsem.at[t])

    @pl.loop(0, tiles)
    def _(t):
        start_all(gate_load(t))

    @pl.loop(0, tiles)
    def _(t):
        down_load(t).start()

    osend[...] = o_ref[...].astype(bf16)
    barrier = pltpu.get_barrier_semaphore()
    mem.greet(barrier)
    hw.greet(barrier)
    pl.semaphore_wait(barrier, n - 1 + nh - 1)

    ca = mem.copies(
        lambda p: st_ref.at[p], lambda d: strecv.at[d - 1], lambda i: sa.at[i], lambda i: ra.at[i]
    )
    cb = mem.copies(
        lambda p: osend.at[p], lambda d: orecv.at[d - 1], lambda i: sb.at[i], lambda i: rb.at[i]
    )
    start_all(ca)
    start_all(cb)
    recv_all(ca)

    def spread(x):
        return jnp.broadcast_to(x[0:1], (LANES, per)).T

    stats = [spread(st_ref[mem.me])] + [spread(strecv[d]) for d in range(n - 1)]
    top = functools.reduce(jnp.maximum, stats)
    weights = [jnp.exp(x - top) for x in stats]
    total = functools.reduce(lambda a, b: a + b, weights)
    recv_all(cb)
    acc = o_ref[mem.me] * weights[0]
    for d in range(n - 1):
        acc = acc + orecv[d].astype(f32) * weights[d + 1]
    flat[...] = acc / total
    for h in range(q_here):
        att[mem.me, :, h * LANES : (h + 1) * LANES] = flat[pl.ds(h, rn, stride=q_here), :].astype(
            bf16
        )
    cc = mem.copies(
        lambda p: att.at[mem.me], lambda d: att.at[mem.me], lambda i: sc.at[i], lambda i: rc.at[i]
    )
    start_all(cc)
    load_o.wait()
    recv_all(cc)
    rows = n * rn
    attended = att[...].astype(f32).reshape(rows, att.shape[2]).astype(bf16)

    to = dl if dl % LANES else tile_of(dl, 640)
    for t in range(dl // to):
        block = jnp.dot(attended, wo[:, t * to : (t + 1) * to], preferred_element_type=f32)
        opart[:, :, t * to : (t + 1) * to] = block.reshape(nh, rh_rows, to)
    cd = hw.copies(
        lambda p: opart.at[p], lambda d: orow.at[d - 1], lambda i: sd.at[i], lambda i: rd.at[i]
    )
    start_all(cd)
    recv_all(cd)
    mid = opart[hw.me]
    for d in range(nh - 1):
        mid = mid + orow[d]
    mid = (res_ref[hw.me].astype(f32) + mid).astype(bf16).astype(f32)
    sq[...] = jnp.broadcast_to(jnp.sum(mid * mid, axis=1, keepdims=True), sq.shape)
    ce = mem.copies(lambda p: sq, lambda d: sqr.at[d - 1], lambda i: se.at[i], lambda i: re.at[i])
    start_all(ce)
    recv_all(ce)
    total = sq[...]
    for d in range(n - 1):
        total = total + sqr[d]
    scale = lax.rsqrt(total / (dl * n) + epsilon)[:, :1]
    midn[hw.me] = (mid * scale * gain_ref[...]).astype(bf16)
    cf = hw.copies(
        lambda p: midn.at[hw.me], lambda d: midn.at[hw.me], lambda i: sf.at[i], lambda i: rf.at[i]
    )
    start_all(cf)
    recv_all(cf)
    normed = midn[...].astype(f32).reshape(rows, dl).astype(bf16)

    def cg(t):
        return mem.copies(
            lambda p: gsend.at[t, p], lambda d: grecv.at[t, d - 1],
            lambda i: sg.at[t, i], lambda i: rg.at[t, i],
        )

    def ch(t):
        return mem.copies(
            lambda p: act.at[t, mem.me], lambda d: act.at[t, mem.me],
            lambda i: sh.at[t, i], lambda i: rh.at[t, i],
        )

    @pl.loop(0, tiles)
    def _(t):
        for c in gate_load(t):
            c.wait()
        gate = jnp.dot(normed, wg[t], preferred_element_type=f32).reshape(n, rn, tn)
        up = jnp.dot(normed, wu[t], preferred_element_type=f32).reshape(n, rn, tn)
        gown[t, :, 0] = gate
        gown[t, :, 1] = up
        gsend[t, :, 0] = gate.astype(bf16)
        gsend[t, :, 1] = up.astype(bf16)
        start_all(cg(t))

    @pl.loop(0, tiles)
    def _(t):
        recv_all(cg(t))
        both = gown[t, mem.me]
        for d in range(n - 1):
            both = both + grecv[t, d].astype(f32)
        gate, up = both[0], both[1]
        act[t, mem.me] = (gate / (1.0 + jnp.exp(-gate)) * up).astype(bf16)
        start_all(ch(t))

    dpart[...] = jnp.zeros_like(dpart)

    @pl.loop(0, tiles)
    def _(t):
        recv_all(ch(t))
        down_load(t).wait()
        block = act[t].astype(f32).reshape(rows, tn).astype(bf16)
        dpart[...] += jnp.dot(block, wd[t], preferred_element_type=f32).reshape(dpart.shape)

    ci = hw.copies(
        lambda p: dpart.at[p], lambda d: drecv.at[d - 1], lambda i: si.at[i], lambda i: ri.at[i]
    )
    start_all(ci)
    recv_all(ci)
    last = dpart[hw.me]
    for d in range(nh - 1):
        last = last + drecv[d]
    fin[hw.me] = (mid + last).astype(bf16)
    cj = hw.copies(
        lambda p: fin.at[hw.me], lambda d: fin.at[hw.me], lambda i: sj.at[i], lambda i: rj.at[i]
    )
    start_all(cj)
    recv_all(cj)
    out_ref[...] = fin[...]
    send_all(ca + cb + cc + cd + ce + cf + ci + cj)

    @pl.loop(0, tiles)
    def _(t):
        send_all(cg(t))
        send_all(ch(t))


def per_device(
    n, hwn,
    residual_in, attention_gain, query_weight, key_weight, value_weight, query_norm, key_norm,
    cache_keys, cache_values, slot_request, lengths, output_weight, second_gain, gate_weight,
    up_weight, down_weight,
):
    rows, dl = residual_in.shape
    requests = rows // 2
    hd = query_norm.shape[0]
    cap, kv, _ = cache_keys.shape
    q_here = query_weight.shape[1] // hd
    nh = math.prod(hwn)
    rn, rh = rows // n, rows // nh
    cq, ck = query_weight.shape[1], key_weight.shape[1]
    cols = cq + 2 * ck
    VM = pl.BlockSpec(memory_space=pltpu.VMEM)
    SM = pl.BlockSpec(memory_space=pltpu.SMEM)
    ANY = pl.BlockSpec(memory_space=pl.ANY)
    DMA = pltpu.SemaphoreType.DMA

    offsets = jnp.arange(2, dtype=jnp.int32)
    places = (lengths[:, None] + offsets[None, :]).reshape(rows).astype(f32)
    half = hd // 2
    frequency = rope_base ** (-(jnp.arange(half, dtype=f32) * 2.0) / hd)
    angles = places[:, None] * frequency
    cosine, sine = jnp.cos(angles), jnp.sin(angles)
    cos2 = jnp.concatenate([cosine, cosine], axis=1)
    sin2 = jnp.concatenate([-sine, sine], axis=1)
    ids = jnp.arange(requests, dtype=jnp.int32)
    starts = jnp.sum((slot_request[None, :] < ids[:, None]).astype(jnp.int32), axis=1)
    ends = jnp.sum((slot_request[None, :] <= ids[:, None]).astype(jnp.int32), axis=1)

    qkv = pl.pallas_call(
        functools.partial(qkv_kernel, n, q_here, kv),
        out_shape=jax.ShapeDtypeStruct((n, rn, cols), bf16),
        in_specs=[VM] * 6 + [ANY] * 3,
        out_specs=VM,
        scratch_shapes=[
            pltpu.VMEM((dl, cols), bf16),
            pltpu.VMEM((rows, LANES), f32),
            pltpu.VMEM((n - 1, rows, LANES), f32),
            pltpu.VMEM((n, rn, cols), f32),
            pltpu.VMEM((n - 1, rn, cols), f32),
            pltpu.VMEM((n, rn, cols), bf16),
            DMA((3,)),
        ]
        + [DMA((n - 1,))] * 6,
        compiler_params=pltpu.CompilerParams(
            collective_id=0, has_side_effects=True, vmem_limit_bytes=VMEM_LIMIT
        ),
        name="qkv",
    )(
        residual_in, attention_gain[None, :], query_norm[None, :], key_norm[None, :], cos2, sin2,
        query_weight, key_weight, value_weight,
    )
    flat = qkv.reshape(rows, cols)
    m_rows = 2 * q_here
    queries = flat[:, :cq].reshape(requests, m_rows, hd)
    new_keys = flat[:, cq : cq + ck].reshape(requests, 2 * kv, hd).astype(f32)
    new_values = flat[:, cq + ck :].reshape(requests, 2 * kv, hd).astype(f32)

    rpc = requests // n
    per = rpc * m_rows
    partial, stats = pl.pallas_call(
        functools.partial(attend_kernel, n, kv),
        out_shape=(
            jax.ShapeDtypeStruct((requests, m_rows, hd), f32),
            jax.ShapeDtypeStruct((n, 8, per), f32),
        ),
        in_specs=[SM, SM] + [VM] * 5,
        out_specs=(VM, VM),
        scratch_shapes=[pltpu.VMEM((requests, m_rows, LANES), f32)],
        compiler_params=pltpu.CompilerParams(vmem_limit_bytes=VMEM_LIMIT),
        name="attend",
    )(
        starts, ends, queries, new_keys, new_values,
        cache_keys.reshape(cap * kv, hd), cache_values.reshape(cap * kv, hd),
    )

    ffl = gate_weight.shape[1]
    tn = tile_of(ffl, 640)
    tiles = ffl // tn
    mems, hws = DMA((n - 1,)), DMA((nh - 1,))
    tms = DMA((tiles, n - 1))
    out = pl.pallas_call(
        functools.partial(tail_kernel, n, hwn, q_here),
        out_shape=jax.ShapeDtypeStruct((nh, rh, dl), bf16),
        in_specs=[VM] * 4 + [ANY] * 4,
        out_specs=VM,
        scratch_shapes=[
            pltpu.VMEM((cq, dl), bf16),
            pltpu.VMEM((tiles, dl, tn), bf16),
            pltpu.VMEM((tiles, dl, tn), bf16),
            pltpu.VMEM((tiles, tn, dl), bf16),
            pltpu.VMEM((n, per, hd), bf16),
            pltpu.VMEM((n - 1, per, hd), bf16),
            pltpu.VMEM((n - 1, 8, per), f32),
            pltpu.VMEM((per, hd), f32),
            pltpu.VMEM((n, rn, cq), bf16),
            pltpu.VMEM((nh, rh, dl), f32),
            pltpu.VMEM((nh - 1, rh, dl), f32),
            pltpu.VMEM((nh, rh, dl), bf16),
            pltpu.VMEM((rh, LANES), f32),
            pltpu.VMEM((n - 1, rh, LANES), f32),
            pltpu.VMEM((tiles, n, 2, rn, tn), bf16),
            pltpu.VMEM((tiles, n - 1, 2, rn, tn), bf16),
            pltpu.VMEM((tiles, n, 2, rn, tn), f32),
            pltpu.VMEM((tiles, n, rn, tn), bf16),
            pltpu.VMEM((nh, rh, dl), f32),
            pltpu.VMEM((nh - 1, rh, dl), f32),
            pltpu.VMEM((nh, rh, dl), bf16),
            DMA, DMA((tiles,)), DMA((tiles,)), DMA((tiles,)),
            mems, mems, mems, mems, mems, mems, hws, hws, mems, mems, hws, hws,
            tms, tms, tms, tms, hws, hws, hws, hws,
        ],
        compiler_params=pltpu.CompilerParams(
            collective_id=1, has_side_effects=True, vmem_limit_bytes=VMEM_LIMIT
        ),
        name="tail",
    )(
        partial.reshape(n, per, hd), stats, residual_in.reshape(nh, rh, dl), second_gain[None, :],
        output_weight, gate_weight, up_weight, down_weight,
    )
    return out.reshape(rows, dl)


def solution(mesh):
    hwn = (mesh.shape["head"], mesh.shape["width"])
    return jax.shard_map(
        functools.partial(per_device, mesh.shape["mem"], hwn),
        mesh=mesh,
        in_specs=(
            P("groups", "mem"),
            P("mem"),
            P("mem", ("head", "width")),
            P("mem", ("head", "width")),
            P("mem", ("head", "width")),
            P(),
            P(),
            P(("groups", "mem"), ("head", "width"), None),
            P(("groups", "mem"), ("head", "width"), None),
            P(("groups", "mem")),
            P("groups"),
            P(("head", "width"), "mem"),
            P("mem"),
            P("mem", ("head", "width")),
            P("mem", ("head", "width")),
            P(("head", "width"), "mem"),
        ),
        out_specs=P("groups", "mem"),
        check_vma=False,
    )
```
